32 devices in a mesh: cent: 8 (over y, x, core), rep: 4 (over z).
Axes of the slice: x: 2, y: 2, z: 4, core: 2. Of those that a mesh axis runs over, the one named last changes fastest.
Arguments:
- points: bfloat16 [16384, 1024], P(('cent', 'rep')), may hold values from -6 to 6
- centroids: bfloat16 [4096, 1024], P('cent'), may hold values from -6 to 6
- owners: int32 [16384, 2], P(('cent', 'rep')), may hold values from 0 to 7, all different within a row; in each aligned block of 512 rows (0 to 511, 512 to 1023, ...) at most 320 rows name the same one
- blocks: int32 [16384, 2, 4], P(('cent', 'rep')), may hold values from 0 to 7, all different within a row
- duals: float32 [4096], P('cent'), may hold values from -1 to 1
Outputs:
- new_centroids: bfloat16 [4096, 1024], P('cent')
- duals_out: float32 [4096], P('cent')
The draws below stay inside these ranges and needn't reach their ends.
Inputs may be any that keep to these rules, and one draw needn't show every extreme that they name: `owners`: each point names 2 different owner shards; among the points of one device no shard is named more than 320 times, a bound that some block reaches. `blocks`: the 4 block numbers that a point names within one owner shard differ.
All inputs are finite; a program needn't handle non-finite values.
Results may differ from the reference program's by a relative error of at most 0.012.
The reference program's roundings to bfloat16 on the way count: a program that leaves them out, or rounds other values in their place, can miss the bound.
Values may be sent and summed in bfloat16 or wider, within the bound.
A program may use at most 64 MiB of HBM per device.

```python
import math
import jax
import jax.numpy as jnp
import numpy as np
from jax import lax

EMBED_WIDTH = 1024
P_DEV = 512
K_DEV = 512
BLOCKS_DEV = 8
CAND = 4
ROUTES = 2
SINK = 3
ITERS = 2
SHARDS = 8
CAP = 320
POINTS = 16384
CLUSTERS = 4096
N_CENT = 8
N_REP = 4


def block_scale(rng, extent, pieces, least, high):
    factor_of = 1.0
    for axis_at, shards_of in pieces:
        draws = jax.random.uniform(jax.random.fold_in(jax.random.fold_in(rng, 6), axis_at), (shards_of,), jnp.float32, least / len(pieces), high / len(pieces))
        factor_of = factor_of * jnp.repeat(jnp.exp(draws), extent[axis_at] // shards_of).reshape((-1,) + (1,) * (len(extent) - 1 - axis_at))
    return factor_of


def distinct(own_key, rows, number_of, top, lift):
    ranking = jax.random.permutation(jax.random.fold_in(own_key, 1), number_of)
    boost = ranking
    for power in range(3):
        boost = boost * boost // number_of
    boost = boost * lift // number_of
    lots = jax.random.randint(jax.random.fold_in(own_key, 2), (rows, number_of), 0, 4096) + boost
    holders = jax.random.permutation(jax.random.fold_in(own_key, 3), rows)[jnp.arange(number_of) % rows]
    lots = jnp.where(jnp.arange(rows)[:, None] == holders[None, :], 1 << 14, lots)
    merit = lots * number_of + jnp.arange(number_of)
    return lax.top_k(merit.astype(jnp.int32), top)[1].astype(jnp.int32)


def deal_out(rng, own, number, rows, count, top, most, lean):
    order = jax.random.permutation(rng, count)
    crowded, common = shares(count, rows * top, most, lean, True), shares(count, rows * top, most, lean, False)
    places = jnp.arange(count)

    def named(tallies, rotation):
        used = int((tallies > 0).sum())
        fixed = max(1, used // 4)
        shifted = fixed + (places - fixed + rotation * (used - fixed)) % max(1, count - fixed)
        return jnp.zeros((count,), jnp.int32).at[order[jnp.where(places < fixed, places, shifted)]].set(jnp.asarray(tallies, jnp.int32))

    tallies = jnp.where(number % 4 == 0, named(crowded, number // 4), named(common, number - number // 4 - 1))
    mixed = jax.random.permutation(jax.random.fold_in(own, 3), count)
    source_of, taker = mixed[0:count // 2 * 2:2], mixed[1:count // 2 * 2:2]
    room = jnp.minimum(tallies[source_of] - 1, most - tallies[taker]) // 2
    room = jnp.where((source_of == order[0]) | (taker == order[0]) | (tallies[taker] == 0), 0, jnp.maximum(room, 0))
    shifted = jax.random.randint(jax.random.fold_in(own, 4), (count // 2,), 0, 1 << 20) % (room + 1)
    tallies = tallies.at[source_of].add(-shifted).at[taker].add(shifted)
    members = jnp.searchsorted(jnp.cumsum(tallies), jnp.arange(rows * top), side="right").astype(jnp.int32)
    grid = members.reshape(top, rows).T
    grid = grid[jax.random.permutation(jax.random.fold_in(own, 1), rows)]
    rotation = jax.random.randint(jax.random.fold_in(own, 2), (rows, 1), 0, top)
    return jnp.take_along_axis(grid, (jnp.arange(top)[None, :] + rotation) % top, axis=1)


def shares(amount, total, most, slope, full):
    loads = [(1 << 20) // math.isqrt(grade ** slope) + 1 for grade in range(1, amount + 1)]
    largest = most if full else min(most, max(-(-total // amount), total * loads[0] // sum(loads)))
    least = 1 if total - largest >= amount - 1 else 0
    counts, spare = [largest] + [least] * (amount - 1), total - largest - least * (amount - 1)
    while spare > 0:
        free = [i for i in range(1, amount) if counts[i] < largest] or [i for i in range(1, amount) if counts[i] < most]
        pool, left = sum([loads[i] for i in free]), spare
        for i in free:
            extra = min(most - counts[i], max(1, left * loads[i] // pool), spare)
            counts[i] = counts[i] + extra
            spare = spare - extra
    return np.array(counts)


def bell_draw(rng, shape, deviation, bound, split=(), held_as=jnp.bfloat16):
    entries = jax.random.normal(rng, shape, jnp.float32) * deviation
    if len(split) > 0:
        entries = block_scale(rng, shape, split, -0.22, 0.18) * entries
    return jnp.clip(entries, min=-bound, max=bound).astype(held_as)


def setup_inputs(seed: int = 0) -> dict:
    arg_keys = jax.random.split(jax.random.key(seed), 6)
    points = bell_draw(arg_keys[0], (POINTS, EMBED_WIDTH), 1.0, 6.0, ((0, 32),))
    centroids = bell_draw(arg_keys[1], (CLUSTERS, EMBED_WIDTH), 1.0, 6.0, ((0, 8),))
    owners_keys = jax.random.split(jax.random.fold_in(arg_keys[2], 1), POINTS // P_DEV)
    owners_turns = jax.random.permutation(jax.random.fold_in(arg_keys[2], 3), POINTS // P_DEV)
    owners = jax.vmap(lambda own, number: deal_out(jax.random.fold_in(arg_keys[2], 2), own, number, P_DEV, SHARDS, ROUTES, CAP, 1))(owners_keys, owners_turns).reshape((POINTS, ROUTES))
    blocks = distinct(arg_keys[3], POINTS * ROUTES, BLOCKS_DEV, CAND, 0).reshape((POINTS, ROUTES, CAND))
    duals = jnp.clip(jax.random.uniform(arg_keys[4], (CLUSTERS,), jnp.float32, -1.0, 1.0) * block_scale(arg_keys[4], (CLUSTERS,), ((0, 8),), -0.4, 0.0), -1.0, 1.0)
    return {"points": points, "centroids": centroids, "owners": owners, "blocks": blocks, "duals": duals}


softness_factor = 0.02
EPSILON = 1e-06

def normalize(values):
    widened = values.astype(jnp.float32)
    return (widened * lax.rsqrt(lax.optimization_barrier(jnp.mean(widened * widened, axis=-1, keepdims=True)) + EPSILON)).astype(jnp.bfloat16)

def reference(points, centroids, owners, blocks, duals):
    total_points = points.shape[0]
    route_count = total_points * ROUTES
    block_span = K_DEV // BLOCKS_DEV
    per_owner = N_CENT * N_REP * CAP
    target = P_DEV * N_REP / K_DEV
    unit_rows = normalize(points)
    flat_owner = owners.reshape(-1).astype(jnp.int32)
    flat_point = jnp.arange(route_count, dtype=jnp.int32) // ROUTES
    flat_blocks = blocks.reshape(route_count, CAND).astype(jnp.int32)
    shard_ids = jnp.arange(N_CENT, dtype=jnp.int32)
    owner_loads = lax.optimization_barrier(jnp.sum((flat_owner[None, :] == shard_ids[:, None]).astype(jnp.int32), axis=1))
    starts = jnp.cumsum(owner_loads) - owner_loads
    ordering = jnp.argsort(flat_owner, stable=True).astype(jnp.int32)
    offsets = jnp.arange(per_owner, dtype=jnp.int32)
    live_slots = offsets[None, :] < owner_loads[:, None]
    picked = ordering[jnp.clip(starts[:, None] + offsets[None, :], 0, route_count - 1)]
    picked = jnp.where(live_slots, picked, 0).astype(jnp.int32)
    member = jnp.any(flat_blocks[picked][:, :, :, None] == jnp.arange(BLOCKS_DEV, dtype=jnp.int32), axis=2)
    member = jnp.logical_and(member, live_slots[:, :, None]).astype(jnp.float32)
    live_float = live_slots.astype(jnp.float32)
    current = centroids
    duals_now = duals.reshape(N_CENT, K_DEV).astype(jnp.float32)
    for loop_counter in range(ITERS):
        centroid_unit = normalize(current).reshape(N_CENT, K_DEV, EMBED_WIDTH)

        def owner_kernel(inputs):
            chosen, block_marks, center_rows = inputs
            collected_rows = unit_rows[flat_point[chosen]]
            affinity_scores = lax.dot_general(collected_rows, center_rows, (((1,), (1,)), ((), ())), preferred_element_type=jnp.float32) / (EMBED_WIDTH * softness_factor)
            return jnp.exp(affinity_scores) * jnp.repeat(block_marks, block_span, axis=1)
        kernel = lax.map(owner_kernel, (picked, member, centroid_unit))
        for turn_index in range(SINK + 1):
            scaling = jnp.exp(duals_now)
            partial_rows = jnp.einsum('crk,ck->cr', kernel, scaling, precision=lax.Precision.HIGHEST)
            route_parts = jnp.zeros((route_count,), jnp.float32).at[picked.reshape(-1)].add(partial_rows.reshape(-1))
            inverse = 1.0 / lax.optimization_barrier(jnp.sum(route_parts.reshape(total_points, ROUTES), axis=1))
            row_scale = inverse[flat_point[picked]] * live_float
            if turn_index < SINK:
                column_mass = jnp.einsum('cr,crk->ck', row_scale, kernel, precision=lax.Precision.HIGHEST) * scaling
                duals_now = duals_now + jnp.log(2.0 * target) - jnp.log(column_mass + target)
        weights = (row_scale[:, :, None] * kernel * scaling[:, None, :]).astype(jnp.bfloat16)

        def owner_sums(inputs):
            chosen, weight_rows = inputs
            collected_rows = unit_rows[flat_point[chosen]]
            return lax.dot_general(weight_rows, collected_rows, (((0,), (0,)), ((), ())), preferred_element_type=jnp.float32)
        summed = lax.map(owner_sums, (picked, weights)).reshape(N_CENT * K_DEV, EMBED_WIDTH)
        current = normalize(summed)
    return (current, duals_now.reshape(-1))
```

```python
import functools

import jax
import jax.numpy as jnp
from jax import lax
from jax.experimental import pallas as pl
from jax.experimental.pallas import tpu as pltpu
from jax.sharding import PartitionSpec as P

BLOCKS_DEV = 8
CAND = 4
SINK = 3
ITERS = 2
LANES = 128
SUBLANES = 8
MESH = pl.DeviceIdType.MESH
VMEM_LIMIT = 64000000


softness_factor = 0.02
EPSILON = 1e-06


def normalize(values):
    widened = values.astype(jnp.float32)
    return (
        widened * lax.rsqrt(jnp.mean(widened * widened, axis=-1, keepdims=True) + EPSILON)
    ).astype(jnp.bfloat16)


def candidate_mask(labels_in, block_span):
    member = jnp.any(
        labels_in[:, :, None] == jnp.arange(BLOCKS_DEV, dtype=jnp.int32)[None, None, :], axis=1
    )
    return jnp.repeat(member.astype(jnp.float32), block_span, axis=1)


def kernel_of(slot_rows, slot_mask, centroid_unit, feature_dimension):
    affinity_scores = lax.dot_general(
        slot_rows, centroid_unit, (((1,), (1,)), ((), ())), preferred_element_type=jnp.float32
    ) / (feature_dimension * softness_factor)
    return jnp.exp(affinity_scores) * slot_mask


def routed_body(points, centroids, owners, blocks, duals):
    point_rows, feature_dimension = points.shape
    shard_rows = centroids.shape[0]
    shards = lax.axis_size("cent")
    replicas = lax.axis_size("rep")
    routes = owners.shape[1]
    capacity = 5 * point_rows // shards
    block_span = shard_rows // BLOCKS_DEV
    target = point_rows * replicas / shard_rows
    unit_rows = normalize(points)
    flat_owner = owners.reshape(-1)
    flat_point = jnp.arange(point_rows * routes, dtype=jnp.int32) // routes
    onehot = (flat_owner[:, None] == jnp.arange(shards, dtype=jnp.int32)[None, :]).astype(jnp.int32)
    position = jnp.sum((jnp.cumsum(onehot, axis=0) - onehot) * onehot, axis=1)
    outgoing = (
        jnp.zeros((shards, capacity, feature_dimension), jnp.bfloat16)
        .at[flat_owner, position]
        .set(unit_rows[flat_point])
    )
    labels = (
        jnp.full((shards, capacity, CAND), -1, jnp.int32)
        .at[flat_owner, position]
        .set(blocks.reshape(-1, CAND))
    )
    first_unit = normalize(centroids)
    received_rows = (
        lax.all_to_all(outgoing, "cent", split_axis=0, concat_axis=0, tiled=True),
        lax.all_to_all(labels, "cent", split_axis=0, concat_axis=0, tiled=True),
    )
    slot_rows = received_rows[0].reshape(-1, feature_dimension)
    slot_mask = candidate_mask(received_rows[1].reshape(-1, CAND), block_span)
    first_kernel = kernel_of(slot_rows, slot_mask, first_unit, feature_dimension)
    current = centroids
    duals_now = duals
    for loop_counter in range(ITERS):
        if loop_counter == 0:
            kernel = first_kernel
        else:
            kernel = kernel_of(slot_rows, slot_mask, normalize(current), feature_dimension)
        for turn_index in range(SINK + 1):
            scaling = jnp.exp(duals_now)
            partial_rows = jnp.dot(kernel, scaling, precision=lax.Precision.HIGHEST).reshape(
                shards, capacity
            )
            returned = lax.all_to_all(partial_rows, "cent", split_axis=0, concat_axis=0, tiled=True)
            totals = jnp.sum(returned[flat_owner, position].reshape(point_rows, routes), axis=1)
            inverse = 1.0 / totals
            spread = (
                jnp.zeros((shards, capacity), jnp.float32)
                .at[flat_owner, position]
                .set(inverse[flat_point])
            )
            row_scale = lax.all_to_all(
                spread, "cent", split_axis=0, concat_axis=0, tiled=True
            ).reshape(-1)
            if turn_index < SINK:
                local_mass = jnp.dot(row_scale, kernel, precision=lax.Precision.HIGHEST) * scaling
                column_mass = lax.psum(local_mass, "rep")
                duals_now = duals_now + jnp.log(2.0 * target) - jnp.log(column_mass + target)
        weights = (row_scale[:, None] * kernel * scaling[None, :]).astype(jnp.bfloat16)
        share_sums = lax.psum_scatter(
            lax.dot_general(
                weights, slot_rows, (((0,), (0,)), ((), ())), preferred_element_type=jnp.float32
            ),
            "rep",
            scatter_dimension=0,
            tiled=True,
        )
        current = lax.all_gather(normalize(share_sums), "rep", axis=0, tiled=True)
    return (current, duals_now)


def fused_kernel(
    dims,
    points_ref,
    centroids_ref,
    mask_ref,
    duals_ref,
    out_ref,
    duals_out_ref,
    units,
    masks,
    kern,
    cunit,
    scale_cols,
    mass_cols,
    sums,
    row_parts,
    col_parts,
    sums_out,
    sums_in,
    unit_send,
    unit_recv,
    mask_send,
    mask_recv,
    row_send,
    row_recv,
    col_send,
    col_recv,
    sum_send,
    sum_recv,
    new_send,
    new_recv,
):
    shards, replicas, point_rows, shard_rows, features = dims
    span = shard_rows // BLOCKS_DEV
    pieces = 4
    piece = point_rows // pieces
    dual_rows = shard_rows // LANES
    share = shard_rows // replicas
    target = point_rows * replicas / shard_rows
    inverse_soft = 1.0 / (features * softness_factor)

    me = lax.axis_index("cent")
    z = lax.axis_index("rep")
    core = me % 2
    xpos = (me // 2) % 2
    ypos = me // 4

    def rel(direction):
        dc, dx, dy = direction % 2, (direction // 2) % 2, direction // 4
        c = 1 - core if dc else core
        x = 1 - xpos if dx else xpos
        y = 1 - ypos if dy else ypos
        return (y * 2 + x) * 2 + c

    peer = [rel(d) for d in range(shards)]
    zpeer = [(z + k) % replicas for k in range(replicas)]

    barrier = pltpu.get_barrier_semaphore()
    for d in range(1, shards):
        pl.semaphore_signal(barrier, inc=1, device_id=(peer[d], z), device_id_type=MESH)
    for k in range(1, replicas):
        pl.semaphore_signal(barrier, inc=1, device_id=(me, zpeer[k]), device_id_type=MESH)
    pl.semaphore_wait(barrier, shards - 1 + replicas - 1)

    mask_copies = []
    for d in range(1, shards):
        copy = pltpu.make_async_remote_copy(
            src_ref=mask_ref.at[peer[d]],
            dst_ref=masks.at[d],
            send_sem=mask_send.at[d],
            recv_sem=mask_recv.at[d],
            device_id=(peer[d], z),
            device_id_type=MESH,
        )
        copy.start()
        mask_copies.append(copy)
    masks[0] = mask_ref[me]

    unit_copies = {}

    def push(slot, chunk, direction):
        rows = pl.ds(chunk * piece, piece)
        copy = pltpu.make_async_remote_copy(
            src_ref=units.at[slot, rows],
            dst_ref=units.at[slot ^ direction, rows],
            send_sem=unit_send.at[slot, chunk, direction // 2],
            recv_sem=unit_recv.at[slot ^ direction, chunk],
            device_id=(peer[direction], z),
            device_id_type=MESH,
        )
        copy.start()
        unit_copies[(slot, chunk, direction)] = copy

    def arrive(slot, chunk):
        rows = pl.ds(chunk * piece, piece)
        pltpu.make_async_copy(
            units.at[slot, rows], units.at[slot, rows], unit_recv.at[slot, chunk]
        ).wait()

    order_x = (0, 1, 2, 3)
    order_y = (2, 3, 0, 1)
    for step in (0, 2, 1, 3):
        rows = pl.ds(step * piece, piece)
        units[0, rows] = normalize(points_ref[rows])
        if step == 0:
            push(0, 0, 2)
        if step == 2:
            push(0, 2, 4)
        if step == 1:
            push(0, 1, 2)
            push(0, 2, 2)
        if step == 3:
            push(0, 3, 4)
            push(0, 3, 2)
            push(0, 0, 4)
            push(0, 1, 4)
    for step in range(pieces):
        push(0, step, 1)

    cunit[...] = normalize(centroids_ref[...])

    def block_kernel(slot):
        scores = lax.dot_general(
            cunit[...],
            units[slot],
            (((1,), (1,)), ((), ())),
            preferred_element_type=jnp.float32,
        )
        marks = masks[slot]
        for b in range(BLOCKS_DEV):
            rows = slice(b * span, (b + 1) * span)
            kern[slot, rows, :] = jnp.exp(scores[rows] * inverse_soft) * marks[b : b + 1, :]

    block_kernel(0)
    for step in range(pieces):
        tx, ty = order_x[step], order_y[step]
        arrive(2, tx)
        if step < 2:
            push(2, tx, 4)
        push(2, tx, 1)
        arrive(4, ty)
        if step < 2:
            push(4, ty, 2)
        push(4, ty, 1)
        if step == 1:
            for copy in mask_copies:
                copy.wait()
            for chunk in range(pieces):
                arrive(1, chunk)
            block_kernel(1)
        if step >= 2:
            arrive(6, order_x[step - 2])
            push(6, order_x[step - 2], 1)
            arrive(6, order_y[step - 2])
            push(6, order_y[step - 2], 1)
    for slot in (2, 4, 6, 3, 5, 7):
        if slot % 2:
            for chunk in range(pieces):
                arrive(slot, chunk)
        block_kernel(slot)
    for copy in unit_copies.values():
        copy.wait_send()

    duals_now = duals_ref[...]
    groups = shard_rows // SUBLANES
    tiles = point_rows // LANES

    def spread_scale(scaling):
        for t in range(dual_rows):
            row = jnp.broadcast_to(scaling[t : t + 1, :], (LANES, LANES))
            scale_cols[pl.ds(t * LANES, LANES), :] = row.T

    def row_pass():
        def step(g, acc):
            rows = pl.ds(pl.multiple_of(g * SUBLANES, SUBLANES), SUBLANES)
            wide = jnp.concatenate([scale_cols[rows, :]] * tiles, axis=1)
            return tuple(acc[p] + kern[p, rows, :] * wide for p in range(shards))

        zero = jnp.zeros((SUBLANES, point_rows), jnp.float32)
        acc = lax.fori_loop(0, groups, step, (zero,) * shards, unroll=2)
        return jnp.concatenate([jnp.sum(a, axis=0, keepdims=True) for a in acc], axis=0)

    def col_pass(inverse):
        wide = [
            jnp.broadcast_to(inverse[p : p + 1, :], (SUBLANES, point_rows)) for p in range(shards)
        ]

        def step(g, carry):
            rows = pl.ds(pl.multiple_of(g * SUBLANES, SUBLANES), SUBLANES)
            total = kern[0, rows, :] * wide[0]
            for p in range(1, shards):
                total = total + kern[p, rows, :] * wide[p]
            narrow = total[:, :LANES]
            for t in range(1, tiles):
                narrow = narrow + total[:, t * LANES : (t + 1) * LANES]
            mass_cols[rows, :] = narrow
            return carry

        lax.fori_loop(0, groups, step, 0, unroll=2)
        parts = [
            jnp.sum(mass_cols[pl.ds(t * LANES, LANES), :].T, axis=0, keepdims=True)
            for t in range(dual_rows)
        ]
        return jnp.concatenate(parts * (SUBLANES // dual_rows), axis=0)

    def row_exchange(turn, part):
        row_parts[turn, 0] = part
        copies = []
        for d in (6, 7, 2, 4, 3, 5, 1):
            copy = pltpu.make_async_remote_copy(
                src_ref=row_parts.at[turn, 0],
                dst_ref=row_parts.at[turn, d],
                send_sem=row_send.at[turn, d],
                recv_sem=row_recv.at[turn, d],
                device_id=(peer[d], z),
                device_id_type=MESH,
            )
            copy.start()
            copies.append(copy)
        for copy in copies:
            copy.wait()
        rows = []
        for p in range(shards):
            total = part[p : p + 1, :]
            for d in range(1, shards):
                total = total + row_parts[turn, d, pl.ds(p ^ d, 1), :]
            rows.append(total)
        return jnp.concatenate(rows, axis=0)

    def col_exchange(turn, part):
        col_parts[turn, z] = part
        copies = []
        for k in range(1, replicas):
            copy = pltpu.make_async_remote_copy(
                src_ref=col_parts.at[turn, z],
                dst_ref=col_parts.at[turn, z],
                send_sem=col_send.at[turn, k],
                recv_sem=col_recv.at[turn, k],
                device_id=(me, zpeer[k]),
                device_id_type=MESH,
            )
            copy.start()
            copies.append(copy)
        for copy in copies:
            copy.wait()
        total = col_parts[turn, 0]
        for k in range(1, replicas):
            total = total + col_parts[turn, k]
        return total

    row_turn = 0
    col_turn = 0
    for loop_counter in range(ITERS):
        last = loop_counter == ITERS - 1
        if loop_counter > 0:

            def remake(slot, carry):
                block_kernel(slot)
                return carry

            lax.fori_loop(0, shards, remake, 0)
        for turn_index in range(SINK + 1):
            scaling = jnp.exp(duals_now)
            spread_scale(scaling)
            inverse = 1.0 / row_exchange(row_turn, row_pass())
            row_turn += 1
            if turn_index < SINK:
                mass = col_exchange(col_turn, col_pass(inverse) * scaling)
                col_turn += 1
                duals_now = duals_now + jnp.log(2.0 * target) - jnp.log(mass + target)

        row_parts[row_turn - 1, 0] = inverse

        def accumulate(slot, carry):
            inv = row_parts[row_turn - 1, 0, pl.ds(slot, 1), :]
            wide = jnp.concatenate([scale_cols[...]] * tiles, axis=1)
            weights = (inv * kern[slot] * wide).astype(jnp.bfloat16)
            product = jnp.dot(weights, units[slot], preferred_element_type=jnp.float32)

            @pl.when(slot == 0)
            def _():
                sums[...] = product

            @pl.when(slot > 0)
            def _():
                sums[...] += product

            return carry

        lax.fori_loop(0, shards, accumulate, 0)
        copies = []
        for k in range(1, replicas):
            rows = pl.ds(pl.multiple_of(zpeer[k] * share, share), share)
            sums_out[loop_counter, k] = sums[rows, :].astype(jnp.bfloat16)
            copy = pltpu.make_async_remote_copy(
                src_ref=sums_out.at[loop_counter, k],
                dst_ref=sums_in.at[loop_counter, k],
                send_sem=sum_send.at[loop_counter, k],
                recv_sem=sum_recv.at[loop_counter, k],
                device_id=(me, zpeer[k]),
                device_id_type=MESH,
            )
            copy.start()
            copies.append(copy)
        for copy in copies:
            copy.wait()
        mine = pl.ds(pl.multiple_of(z * share, share), share)
        total = sums[mine, :]
        for k in range(1, replicas):
            total = total + sums_in[loop_counter, k].astype(jnp.float32)
        fresh = normalize(total)
        if last:
            dest = out_ref
        else:
            dest = cunit
            fresh = normalize(fresh)
        dest[mine, :] = fresh
        copies = []
        for k in range(1, replicas):
            copy = pltpu.make_async_remote_copy(
                src_ref=dest.at[mine],
                dst_ref=dest.at[mine],
                send_sem=new_send.at[loop_counter, k],
                recv_sem=new_recv.at[loop_counter, k],
                device_id=(me, zpeer[k]),
                device_id_type=MESH,
            )
            copy.start()
            copies.append(copy)
        for copy in copies:
            copy.wait()
    duals_out_ref[...] = duals_now


def fused_body(points, centroids, owners, blocks, duals):
    point_rows, features = points.shape
    shard_rows = centroids.shape[0]
    shards = lax.axis_size("cent")
    replicas = lax.axis_size("rep")
    dims = (shards, replicas, point_rows, shard_rows, features)
    dual_rows = shard_rows // LANES
    share = shard_rows // replicas
    wanted = owners.T[None, None, :, None, :] == jnp.arange(shards, dtype=jnp.int32).reshape(
        -1, 1, 1, 1, 1
    )
    named = jnp.transpose(blocks, (1, 2, 0))[None, None] == jnp.arange(
        BLOCKS_DEV, dtype=jnp.int32
    ).reshape(1, -1, 1, 1, 1)
    mask = jnp.any(jnp.logical_and(wanted, named), axis=(2, 3)).astype(jnp.float32)
    dual_tile = jnp.concatenate([duals.reshape(dual_rows, LANES)] * (SUBLANES // dual_rows), axis=0)
    vmem = pl.BlockSpec(memory_space=pltpu.VMEM)
    row_turns = ITERS * (SINK + 1)
    col_turns = ITERS * SINK
    dma = pltpu.SemaphoreType.DMA
    new_centroids, duals_out = pl.pallas_call(
        functools.partial(fused_kernel, dims),
        out_shape=(
            jax.ShapeDtypeStruct((shard_rows, features), jnp.bfloat16),
            jax.ShapeDtypeStruct((SUBLANES, LANES), jnp.float32),
        ),
        in_specs=[vmem] * 4,
        out_specs=(vmem, vmem),
        scratch_shapes=[
            pltpu.VMEM((shards, point_rows, features), jnp.bfloat16),
            pltpu.VMEM((shards, BLOCKS_DEV, point_rows), jnp.float32),
            pltpu.VMEM((shards, shard_rows, point_rows), jnp.float32),
            pltpu.VMEM((shard_rows, features), jnp.bfloat16),
            pltpu.VMEM((shard_rows, LANES), jnp.float32),
            pltpu.VMEM((shard_rows, LANES), jnp.float32),
            pltpu.VMEM((shard_rows, features), jnp.float32),
            pltpu.VMEM((row_turns, shards, shards, point_rows), jnp.float32),
            pltpu.VMEM((col_turns, replicas, SUBLANES, LANES), jnp.float32),
            pltpu.VMEM((ITERS, replicas, share, features), jnp.bfloat16),
            pltpu.VMEM((ITERS, replicas, share, features), jnp.bfloat16),
            dma((shards, 4, 3)),
            dma((shards, 4)),
            dma((shards,)),
            dma((shards,)),
            dma((row_turns, shards)),
            dma((row_turns, shards)),
            dma((col_turns, replicas)),
            dma((col_turns, replicas)),
            dma((ITERS, replicas)),
            dma((ITERS, replicas)),
            dma((ITERS, replicas)),
            dma((ITERS, replicas)),
        ],
        compiler_params=pltpu.CompilerParams(
            collective_id=0, has_side_effects=True, vmem_limit_bytes=VMEM_LIMIT
        ),
        name="fused_kmeans",
    )(points, centroids, mask, dual_tile)
    return new_centroids, duals_out[:dual_rows].reshape(shard_rows)


def solution(mesh):
    shards = mesh.shape["cent"]

    def body(points, centroids, owners, blocks, duals):
        point_rows, features = points.shape
        shard_rows = centroids.shape[0]
        plane_bytes = shards * point_rows * (2 * features + 4 * shard_rows)
        cube = shards == 2**3 and shard_rows % LANES == 0 and SUBLANES % (shard_rows // LANES) == 0
        if cube and plane_bytes <= VMEM_LIMIT // 3:
            return fused_body(points, centroids, owners, blocks, duals)
        return routed_body(points, centroids, owners, blocks, duals)

    return jax.shard_map(
        body,
        mesh=mesh,
        in_specs=(
            P(("cent", "rep"), None),
            P("cent", None),
            P(("cent", "rep"), None),
            P(("cent", "rep"), None, None),
            P("cent"),
        ),
        out_specs=(P("cent", None), P("cent")),
        check_vma=False,
    )
```

```python
import functools

import jax
import jax.numpy as jnp
from jax import lax
from jax.experimental import pallas as pl
from jax.experimental.pallas import tpu as pltpu
from jax.sharding import PartitionSpec as P

BLOCKS_DEV = 8
CAND = 4
SINK = 3
ITERS = 2
LANES = 128
SUBLANES = 8
OUT_PIECES = 4
MESH = pl.DeviceIdType.MESH
VMEM_LIMIT = 64000000


softness_factor = 0.02
EPSILON = 1e-06


def normalize(values):
    widened = values.astype(jnp.float32)
    return (
        widened * lax.rsqrt(jnp.mean(widened * widened, axis=-1, keepdims=True) + EPSILON)
    ).astype(jnp.bfloat16)


def candidate_mask(labels_in, block_span):
    member = jnp.any(
        labels_in[:, :, None] == jnp.arange(BLOCKS_DEV, dtype=jnp.int32)[None, None, :], axis=1
    )
    return jnp.repeat(member.astype(jnp.float32), block_span, axis=1)


def kernel_of(slot_rows, slot_mask, centroid_unit, feature_dimension):
    affinity_scores = lax.dot_general(
        slot_rows, centroid_unit, (((1,), (1,)), ((), ())), preferred_element_type=jnp.float32
    ) / (feature_dimension * softness_factor)
    return jnp.exp(affinity_scores) * slot_mask


def routed_body(points, centroids, owners, blocks, duals):
    point_rows, feature_dimension = points.shape
    shard_rows = centroids.shape[0]
    shards = lax.axis_size("cent")
    replicas = lax.axis_size("rep")
    routes = owners.shape[1]
    capacity = 5 * point_rows // shards
    block_span = shard_rows // BLOCKS_DEV
    target = point_rows * replicas / shard_rows
    unit_rows = normalize(points)
    flat_owner = owners.reshape(-1)
    flat_point = jnp.arange(point_rows * routes, dtype=jnp.int32) // routes
    onehot = (flat_owner[:, None] == jnp.arange(shards, dtype=jnp.int32)[None, :]).astype(jnp.int32)
    position = jnp.sum((jnp.cumsum(onehot, axis=0) - onehot) * onehot, axis=1)
    outgoing = (
        jnp.zeros((shards, capacity, feature_dimension), jnp.bfloat16)
        .at[flat_owner, position]
        .set(unit_rows[flat_point])
    )
    labels = (
        jnp.full((shards, capacity, CAND), -1, jnp.int32)
        .at[flat_owner, position]
        .set(blocks.reshape(-1, CAND))
    )
    first_unit = normalize(centroids)
    received_rows = (
        lax.all_to_all(outgoing, "cent", split_axis=0, concat_axis=0, tiled=True),
        lax.all_to_all(labels, "cent", split_axis=0, concat_axis=0, tiled=True),
    )
    slot_rows = received_rows[0].reshape(-1, feature_dimension)
    slot_mask = candidate_mask(received_rows[1].reshape(-1, CAND), block_span)
    first_kernel = kernel_of(slot_rows, slot_mask, first_unit, feature_dimension)
    current = centroids
    duals_now = duals
    for loop_counter in range(ITERS):
        if loop_counter == 0:
            kernel = first_kernel
        else:
            kernel = kernel_of(slot_rows, slot_mask, normalize(current), feature_dimension)
        for turn_index in range(SINK + 1):
            scaling = jnp.exp(duals_now)
            partial_rows = jnp.dot(kernel, scaling, precision=lax.Precision.HIGHEST).reshape(
                shards, capacity
            )
            returned = lax.all_to_all(partial_rows, "cent", split_axis=0, concat_axis=0, tiled=True)
            totals = jnp.sum(returned[flat_owner, position].reshape(point_rows, routes), axis=1)
            inverse = 1.0 / totals
            spread = (
                jnp.zeros((shards, capacity), jnp.float32)
                .at[flat_owner, position]
                .set(inverse[flat_point])
            )
            row_scale = lax.all_to_all(
                spread, "cent", split_axis=0, concat_axis=0, tiled=True
            ).reshape(-1)
            if turn_index < SINK:
                local_mass = jnp.dot(row_scale, kernel, precision=lax.Precision.HIGHEST) * scaling
                column_mass = lax.psum(local_mass, "rep")
                duals_now = duals_now + jnp.log(2.0 * target) - jnp.log(column_mass + target)
        weights = (row_scale[:, None] * kernel * scaling[None, :]).astype(jnp.bfloat16)
        share_sums = lax.psum_scatter(
            lax.dot_general(
                weights, slot_rows, (((0,), (0,)), ((), ())), preferred_element_type=jnp.float32
            ),
            "rep",
            scatter_dimension=0,
            tiled=True,
        )
        current = lax.all_gather(normalize(share_sums), "rep", axis=0, tiled=True)
    return (current, duals_now)


def fused_kernel(
    dims,
    points_ref,
    centroids_ref,
    mask_ref,
    duals_ref,
    out_ref,
    duals_out_ref,
    units,
    masks,
    kern,
    cunit,
    scale_cols,
    mass_cols,
    sums,
    row_parts,
    col_parts,
    sums_out,
    sums_in,
    unit_send,
    unit_recv,
    mask_send,
    mask_recv,
    row_send,
    row_recv,
    col_send,
    col_recv,
    sum_send,
    sum_recv,
    new_send,
    new_recv,
):
    shards, replicas, point_rows, shard_rows, features = dims
    span = shard_rows // BLOCKS_DEV
    pieces = 4
    piece = point_rows // pieces
    dual_rows = shard_rows // LANES
    groups_out = OUT_PIECES
    group = shard_rows // groups_out
    cut = group // replicas
    target = point_rows * replicas / shard_rows
    inverse_soft = 1.0 / (features * softness_factor)

    me = lax.axis_index("cent")
    z = lax.axis_index("rep")
    core = me % 2
    xpos = (me // 2) % 2
    ypos = me // 4

    def rel(direction):
        dc, dx, dy = direction % 2, (direction // 2) % 2, direction // 4
        c = 1 - core if dc else core
        x = 1 - xpos if dx else xpos
        y = 1 - ypos if dy else ypos
        return (y * 2 + x) * 2 + c

    peer = [rel(d) for d in range(shards)]
    zpeer = [(z + k) % replicas for k in range(replicas)]

    barrier = pltpu.get_barrier_semaphore()
    for d in range(1, shards):
        pl.semaphore_signal(barrier, inc=1, device_id=(peer[d], z), device_id_type=MESH)
    for k in range(1, replicas):
        pl.semaphore_signal(barrier, inc=1, device_id=(me, zpeer[k]), device_id_type=MESH)
    pl.semaphore_wait(barrier, shards - 1 + replicas - 1)

    mask_copies = []
    for d in range(1, shards):
        copy = pltpu.make_async_remote_copy(
            src_ref=mask_ref.at[peer[d]],
            dst_ref=masks.at[d],
            send_sem=mask_send.at[d],
            recv_sem=mask_recv.at[d],
            device_id=(peer[d], z),
            device_id_type=MESH,
        )
        copy.start()
        mask_copies.append(copy)
    masks[0] = mask_ref[me]

    unit_copies = {}

    def push(slot, chunk, direction):
        rows = pl.ds(chunk * piece, piece)
        copy = pltpu.make_async_remote_copy(
            src_ref=units.at[slot, rows],
            dst_ref=units.at[slot ^ direction, rows],
            send_sem=unit_send.at[slot, chunk, direction // 2],
            recv_sem=unit_recv.at[slot ^ direction, chunk],
            device_id=(peer[direction], z),
            device_id_type=MESH,
        )
        copy.start()
        unit_copies[(slot, chunk, direction)] = copy

    def arrive(slot, chunk):
        rows = pl.ds(chunk * piece, piece)
        pltpu.make_async_copy(
            units.at[slot, rows], units.at[slot, rows], unit_recv.at[slot, chunk]
        ).wait()

    order_x = (0, 1, 2, 3)
    order_y = (2, 3, 0, 1)
    for step in (0, 2, 1, 3):
        rows = pl.ds(step * piece, piece)
        units[0, rows] = normalize(points_ref[rows])
        if step == 0:
            push(0, 0, 2)
        if step == 2:
            push(0, 2, 4)
        if step == 1:
            push(0, 1, 2)
            push(0, 2, 2)
        if step == 3:
            push(0, 3, 4)
            push(0, 3, 2)
            push(0, 0, 4)
            push(0, 1, 4)
    for step in range(pieces):
        push(0, step, 1)

    cunit[...] = normalize(centroids_ref[...])

    def block_kernel(slot, start=0, count=shard_rows):
        scores = lax.dot_general(
            cunit[pl.ds(start, count), :],
            units[slot],
            (((1,), (1,)), ((), ())),
            preferred_element_type=jnp.float32,
        )
        marks = masks[slot]
        for b in range(count // span):
            rows = pl.ds(start + b * span, span)
            mark = marks[start // span + b : start // span + b + 1, :]
            kern[slot, rows, :] = (
                jnp.exp(scores[b * span : (b + 1) * span] * inverse_soft) * mark
            )

    block_kernel(0)
    for step in range(pieces):
        tx, ty = order_x[step], order_y[step]
        arrive(2, tx)
        if step < 2:
            push(2, tx, 4)
        push(2, tx, 1)
        arrive(4, ty)
        if step < 2:
            push(4, ty, 2)
        push(4, ty, 1)
        if step == 1:
            for copy in mask_copies:
                copy.wait()
            for chunk in range(pieces):
                arrive(1, chunk)
            block_kernel(1)
        if step >= 2:
            arrive(6, order_x[step - 2])
            push(6, order_x[step - 2], 1)
            arrive(6, order_y[step - 2])
            push(6, order_y[step - 2], 1)
    for slot in (2, 4, 6, 3, 5, 7):
        if slot % 2:
            for chunk in range(pieces):
                arrive(slot, chunk)
        block_kernel(slot)
    for copy in unit_copies.values():
        copy.wait_send()

    duals_now = duals_ref[...]
    groups = shard_rows // SUBLANES
    tiles = point_rows // LANES

    def spread_scale(scaling):
        for t in range(dual_rows):
            row = jnp.broadcast_to(scaling[t : t + 1, :], (LANES, LANES))
            scale_cols[pl.ds(t * LANES, LANES), :] = row.T

    def row_pass():
        def step(g, acc):
            rows = pl.ds(pl.multiple_of(g * SUBLANES, SUBLANES), SUBLANES)
            wide = jnp.concatenate([scale_cols[rows, :]] * tiles, axis=1)
            return tuple(acc[p] + kern[p, rows, :] * wide for p in range(shards))

        zero = jnp.zeros((SUBLANES, point_rows), jnp.float32)
        acc = lax.fori_loop(0, groups, step, (zero,) * shards, unroll=2)
        return jnp.concatenate([jnp.sum(a, axis=0, keepdims=True) for a in acc], axis=0)

    def col_pass(inverse):
        wide = [
            jnp.broadcast_to(inverse[p : p + 1, :], (SUBLANES, point_rows)) for p in range(shards)
        ]

        def step(g, carry):
            rows = pl.ds(pl.multiple_of(g * SUBLANES, SUBLANES), SUBLANES)
            total = kern[0, rows, :] * wide[0]
            for p in range(1, shards):
                total = total + kern[p, rows, :] * wide[p]
            narrow = total[:, :LANES]
            for t in range(1, tiles):
                narrow = narrow + total[:, t * LANES : (t + 1) * LANES]
            mass_cols[rows, :] = narrow
            return carry

        lax.fori_loop(0, groups, step, 0, unroll=2)
        parts = [
            jnp.sum(mass_cols[pl.ds(t * LANES, LANES), :].T, axis=0, keepdims=True)
            for t in range(dual_rows)
        ]
        return jnp.concatenate(parts * (SUBLANES // dual_rows), axis=0)

    def row_exchange(turn, part):
        row_parts[turn, 0] = part
        copies = []
        for d in (6, 7, 2, 4, 3, 5, 1):
            copy = pltpu.make_async_remote_copy(
                src_ref=row_parts.at[turn, 0],
                dst_ref=row_parts.at[turn, d],
                send_sem=row_send.at[turn, d],
                recv_sem=row_recv.at[turn, d],
                device_id=(peer[d], z),
                device_id_type=MESH,
            )
            copy.start()
            copies.append(copy)
        for copy in copies:
            copy.wait()
        rows = []
        for p in range(shards):
            total = part[p : p + 1, :]
            for d in range(1, shards):
                total = total + row_parts[turn, d, pl.ds(p ^ d, 1), :]
            rows.append(total)
        return jnp.concatenate(rows, axis=0)

    def col_exchange(turn, part):
        col_parts[turn, z] = part
        copies = []
        for k in range(1, replicas):
            copy = pltpu.make_async_remote_copy(
                src_ref=col_parts.at[turn, z],
                dst_ref=col_parts.at[turn, z],
                send_sem=col_send.at[turn, k],
                recv_sem=col_recv.at[turn, k],
                device_id=(me, zpeer[k]),
                device_id_type=MESH,
            )
            copy.start()
            copies.append(copy)
        for copy in copies:
            copy.wait()
        total = col_parts[turn, 0]
        for k in range(1, replicas):
            total = total + col_parts[turn, k]
        return total

    row_turn = 0
    col_turn = 0
    for loop_counter in range(ITERS):
        last = loop_counter == ITERS - 1
        for turn_index in range(SINK + 1):
            scaling = jnp.exp(duals_now)
            spread_scale(scaling)
            inverse = 1.0 / row_exchange(row_turn, row_pass())
            row_turn += 1
            if turn_index < SINK:
                mass = col_exchange(col_turn, col_pass(inverse) * scaling)
                col_turn += 1
                duals_now = duals_now + jnp.log(2.0 * target) - jnp.log(mass + target)

        row_parts[row_turn - 1, 0] = inverse

        dest = out_ref if last else cunit

        def part_rows(i, q):
            start = i * group + q * cut
            if not isinstance(q, int):
                start = pl.multiple_of(start, cut)
            return pl.ds(start, cut)

        def hop(way, src, dst, send_sem, recv_sem):
            return pltpu.make_async_remote_copy(
                src_ref=src,
                dst_ref=dst,
                send_sem=send_sem,
                recv_sem=recv_sem,
                device_id=(me, zpeer[1] if way == 0 else zpeer[replicas - 1]),
                device_id_type=MESH,
            )

        def sum_hop(way, i, q):
            return hop(
                way,
                sums_out.at[loop_counter, way, i, q],
                sums_in.at[loop_counter, way, i, q],
                sum_send.at[loop_counter, way, i, q],
                sum_recv.at[loop_counter, way, i, q],
            )

        def new_hop(way, i, q):
            return hop(
                way,
                dest.at[part_rows(i, q)],
                dest.at[part_rows(i, q)],
                new_send.at[loop_counter, way, i, q],
                new_recv.at[loop_counter, way, i, q],
            )

        def accumulate(i):
            rows = pl.ds(i * group, group)
            wide = jnp.concatenate([scale_cols[rows, :]] * tiles, axis=1)

            def step(slot, acc):
                inv = row_parts[row_turn - 1, 0, pl.ds(slot, 1), :]
                weights = (inv * kern[slot, rows, :] * wide).astype(jnp.bfloat16)
                return acc + jnp.dot(weights, units[slot], preferred_element_type=jnp.float32)

            zero = jnp.zeros((group, features), jnp.float32)
            sums[rows, :] = lax.fori_loop(0, shards, step, zero)

            def first(way, q):
                sums_out[loop_counter, way, i, q] = sums[part_rows(i, q), :].astype(jnp.bfloat16)
                sum_hop(way, i, q).start()

            @pl.when(z == 0)
            def _():
                for q in range(replicas - 1, 0, -1):
                    first(0, q)

            @pl.when(z == replicas - 1)
            def _():
                for q in range(replicas - 1):
                    first(1, q)

        def relay_sums(i):
            def onward(way, q):
                sum_hop(way, i, q).wait_recv()
                total = sums[part_rows(i, q), :] + sums_in[loop_counter, way, i, q].astype(
                    jnp.float32
                )
                sums_out[loop_counter, way, i, q] = total.astype(jnp.bfloat16)
                sum_hop(way, i, q).start()

            for q in range(replicas - 1, 0, -1):
                mirror = replicas - 1 - q

                @pl.when(jnp.logical_and(z > 0, z < q))
                def _():
                    onward(0, q)

                @pl.when(jnp.logical_and(z < replicas - 1, z > mirror))
                def _():
                    onward(1, mirror)

        def finish_sums(i):
            mine = part_rows(i, z)

            @pl.when(z > 0)
            def _():
                sum_hop(0, i, z).wait_recv()
                sums[mine, :] += sums_in[loop_counter, 0, i, z].astype(jnp.float32)

            @pl.when(z < replicas - 1)
            def _():
                sum_hop(1, i, z).wait_recv()
                sums[mine, :] += sums_in[loop_counter, 1, i, z].astype(jnp.float32)

            fresh = normalize(sums[mine, :])
            dest[mine, :] = fresh if last else normalize(fresh)

            @pl.when(z < replicas - 1)
            def _():
                new_hop(0, i, z).start()

            @pl.when(z > 0)
            def _():
                new_hop(1, i, z).start()

        def relay_new(i):
            for q in range(replicas - 1):
                near = replicas - 2 - q
                mirror = replicas - 1 - near

                @pl.when(z > near)
                def _():
                    new_hop(0, i, near).wait_recv()

                @pl.when(jnp.logical_and(z > near, z < replicas - 1))
                def _():
                    new_hop(0, i, near).start()

                @pl.when(z < mirror)
                def _():
                    new_hop(1, i, mirror).wait_recv()

                @pl.when(jnp.logical_and(z < mirror, z > 0))
                def _():
                    new_hop(1, i, mirror).start()

        def remake(i):
            if last:
                return

            def step(slot, carry):
                block_kernel(slot, i * group, group)
                return carry

            lax.fori_loop(0, shards, step, 0)

        for i in range(groups_out):
            accumulate(i)
        stages = (relay_sums, finish_sums, relay_new, remake)
        for step in range(groups_out + len(stages) - 1):
            for lag, stage in enumerate(stages):
                if 0 <= step - lag < groups_out:
                    stage(step - lag)
        for i in range(groups_out):
            for q in range(replicas):

                @pl.when(z < q)
                def _():
                    sum_hop(0, i, q).wait_send()

                @pl.when(z > q)
                def _():
                    sum_hop(1, i, q).wait_send()

                @pl.when(jnp.logical_and(z >= q, z < replicas - 1))
                def _():
                    new_hop(0, i, q).wait_send()

                @pl.when(jnp.logical_and(z <= q, z > 0))
                def _():
                    new_hop(1, i, q).wait_send()

    duals_out_ref[...] = duals_now


def fused_body(points, centroids, owners, blocks, duals):
    point_rows, features = points.shape
    shard_rows = centroids.shape[0]
    shards = lax.axis_size("cent")
    replicas = lax.axis_size("rep")
    dims = (shards, replicas, point_rows, shard_rows, features)
    dual_rows = shard_rows // LANES
    cut = shard_rows // (OUT_PIECES * replicas)
    wanted = owners.T[None, None, :, None, :] == jnp.arange(shards, dtype=jnp.int32).reshape(
        -1, 1, 1, 1, 1
    )
    named = jnp.transpose(blocks, (1, 2, 0))[None, None] == jnp.arange(
        BLOCKS_DEV, dtype=jnp.int32
    ).reshape(1, -1, 1, 1, 1)
    mask = jnp.any(jnp.logical_and(wanted, named), axis=(2, 3)).astype(jnp.float32)
    dual_tile = jnp.concatenate([duals.reshape(dual_rows, LANES)] * (SUBLANES // dual_rows), axis=0)
    vmem = pl.BlockSpec(memory_space=pltpu.VMEM)
    row_turns = ITERS * (SINK + 1)
    col_turns = ITERS * SINK
    dma = pltpu.SemaphoreType.DMA
    new_centroids, duals_out = pl.pallas_call(
        functools.partial(fused_kernel, dims),
        out_shape=(
            jax.ShapeDtypeStruct((shard_rows, features), jnp.bfloat16),
            jax.ShapeDtypeStruct((SUBLANES, LANES), jnp.float32),
        ),
        in_specs=[vmem] * 4,
        out_specs=(vmem, vmem),
        scratch_shapes=[
            pltpu.VMEM((shards, point_rows, features), jnp.bfloat16),
            pltpu.VMEM((shards, BLOCKS_DEV, point_rows), jnp.float32),
            pltpu.VMEM((shards, shard_rows, point_rows), jnp.float32),
            pltpu.VMEM((shard_rows, features), jnp.bfloat16),
            pltpu.VMEM((shard_rows, LANES), jnp.float32),
            pltpu.VMEM((shard_rows, LANES), jnp.float32),
            pltpu.VMEM((shard_rows, features), jnp.float32),
            pltpu.VMEM((row_turns, shards, shards, point_rows), jnp.float32),
            pltpu.VMEM((col_turns, replicas, SUBLANES, LANES), jnp.float32),
            pltpu.VMEM((ITERS, 2, OUT_PIECES, replicas, cut, features), jnp.bfloat16),
            pltpu.VMEM((ITERS, 2, OUT_PIECES, replicas, cut, features), jnp.bfloat16),
            dma((shards, 4, 3)),
            dma((shards, 4)),
            dma((shards,)),
            dma((shards,)),
            dma((row_turns, shards)),
            dma((row_turns, shards)),
            dma((col_turns, replicas)),
            dma((col_turns, replicas)),
            dma((ITERS, 2, OUT_PIECES, replicas)),
            dma((ITERS, 2, OUT_PIECES, replicas)),
            dma((ITERS, 2, OUT_PIECES, replicas)),
            dma((ITERS, 2, OUT_PIECES, replicas)),
        ],
        compiler_params=pltpu.CompilerParams(
            collective_id=0, has_side_effects=True, vmem_limit_bytes=VMEM_LIMIT
        ),
        name="fused_kmeans",
    )(points, centroids, mask, dual_tile)
    return new_centroids, duals_out[:dual_rows].reshape(shard_rows)


def solution(mesh):
    shards = mesh.shape["cent"]

    def body(points, centroids, owners, blocks, duals):
        point_rows, features = points.shape
        shard_rows = centroids.shape[0]
        plane_bytes = shards * point_rows * (2 * features + 4 * shard_rows)
        cube = shards == 2**3 and shard_rows % LANES == 0 and SUBLANES % (shard_rows // LANES) == 0
        if cube and plane_bytes <= VMEM_LIMIT // 3:
            return fused_body(points, centroids, owners, blocks, duals)
        return routed_body(points, centroids, owners, blocks, duals)

    return jax.shard_map(
        body,
        mesh=mesh,
        in_specs=(
            P(("cent", "rep"), None),
            P("cent", None),
            P(("cent", "rep"), None),
            P(("cent", "rep"), None, None),
            P("cent"),
        ),
        out_specs=(P("cent", None), P("cent")),
        check_vma=False,
    )
```

```python
import functools

import jax
import jax.numpy as jnp
from jax import lax
from jax.experimental import pallas as pl
from jax.experimental.pallas import tpu as pltpu
from jax.sharding import PartitionSpec as P

BLOCKS_DEV = 8
CAND = 4
SINK = 3
ITERS = 2
LANES = 128
SUBLANES = 8
OUT_PIECES = 4
MESH = pl.DeviceIdType.MESH
VMEM_LIMIT = 64000000


softness_factor = 0.02
EPSILON = 1e-06


def normalize(values):
    widened = values.astype(jnp.float32)
    return (
        widened * lax.rsqrt(jnp.mean(widened * widened, axis=-1, keepdims=True) + EPSILON)
    ).astype(jnp.bfloat16)


def candidate_mask(labels_in, block_span):
    member = jnp.any(
        labels_in[:, :, None] == jnp.arange(BLOCKS_DEV, dtype=jnp.int32)[None, None, :], axis=1
    )
    return jnp.repeat(member.astype(jnp.float32), block_span, axis=1)


def kernel_of(slot_rows, slot_mask, centroid_unit, feature_dimension):
    affinity_scores = lax.dot_general(
        slot_rows, centroid_unit, (((1,), (1,)), ((), ())), preferred_element_type=jnp.float32
    ) / (feature_dimension * softness_factor)
    return jnp.exp(affinity_scores) * slot_mask


def routed_body(points, centroids, owners, blocks, duals):
    point_rows, feature_dimension = points.shape
    shard_rows = centroids.shape[0]
    shards = lax.axis_size("cent")
    replicas = lax.axis_size("rep")
    routes = owners.shape[1]
    capacity = 5 * point_rows // shards
    block_span = shard_rows // BLOCKS_DEV
    target = point_rows * replicas / shard_rows
    unit_rows = normalize(points)
    flat_owner = owners.reshape(-1)
    flat_point = jnp.arange(point_rows * routes, dtype=jnp.int32) // routes
    onehot = (flat_owner[:, None] == jnp.arange(shards, dtype=jnp.int32)[None, :]).astype(jnp.int32)
    position = jnp.sum((jnp.cumsum(onehot, axis=0) - onehot) * onehot, axis=1)
    outgoing = (
        jnp.zeros((shards, capacity, feature_dimension), jnp.bfloat16)
        .at[flat_owner, position]
        .set(unit_rows[flat_point])
    )
    labels = (
        jnp.full((shards, capacity, CAND), -1, jnp.int32)
        .at[flat_owner, position]
        .set(blocks.reshape(-1, CAND))
    )
    first_unit = normalize(centroids)
    received_rows = (
        lax.all_to_all(outgoing, "cent", split_axis=0, concat_axis=0, tiled=True),
        lax.all_to_all(labels, "cent", split_axis=0, concat_axis=0, tiled=True),
    )
    slot_rows = received_rows[0].reshape(-1, feature_dimension)
    slot_mask = candidate_mask(received_rows[1].reshape(-1, CAND), block_span)
    first_kernel = kernel_of(slot_rows, slot_mask, first_unit, feature_dimension)
    current = centroids
    duals_now = duals
    for loop_counter in range(ITERS):
        if loop_counter == 0:
            kernel = first_kernel
        else:
            kernel = kernel_of(slot_rows, slot_mask, normalize(current), feature_dimension)
        for turn_index in range(SINK + 1):
            scaling = jnp.exp(duals_now)
            partial_rows = jnp.dot(kernel, scaling, precision=lax.Precision.HIGHEST).reshape(
                shards, capacity
            )
            returned = lax.all_to_all(partial_rows, "cent", split_axis=0, concat_axis=0, tiled=True)
            totals = jnp.sum(returned[flat_owner, position].reshape(point_rows, routes), axis=1)
            inverse = 1.0 / totals
            spread = (
                jnp.zeros((shards, capacity), jnp.float32)
                .at[flat_owner, position]
                .set(inverse[flat_point])
            )
            row_scale = lax.all_to_all(
                spread, "cent", split_axis=0, concat_axis=0, tiled=True
            ).reshape(-1)
            if turn_index < SINK:
                local_mass = jnp.dot(row_scale, kernel, precision=lax.Precision.HIGHEST) * scaling
                column_mass = lax.psum(local_mass, "rep")
                duals_now = duals_now + jnp.log(2.0 * target) - jnp.log(column_mass + target)
        weights = (row_scale[:, None] * kernel * scaling[None, :]).astype(jnp.bfloat16)
        share_sums = lax.psum_scatter(
            lax.dot_general(
                weights, slot_rows, (((0,), (0,)), ((), ())), preferred_element_type=jnp.float32
            ),
            "rep",
            scatter_dimension=0,
            tiled=True,
        )
        current = lax.all_gather(normalize(share_sums), "rep", axis=0, tiled=True)
    return (current, duals_now)


def fused_kernel(
    dims,
    points_ref,
    centroids_ref,
    mask_ref,
    duals_ref,
    out_ref,
    duals_out_ref,
    units,
    masks,
    kern,
    cunit,
    scale_cols,
    mass_cols,
    sums,
    row_parts,
    col_parts,
    sums_out,
    sums_in,
    unit_send,
    unit_recv,
    mask_send,
    mask_recv,
    row_send,
    row_recv,
    col_send,
    col_recv,
    sum_send,
    sum_recv,
    new_send,
    new_recv,
):
    shards, replicas, point_rows, shard_rows, features = dims
    span = shard_rows // BLOCKS_DEV
    pieces = 4
    piece = point_rows // pieces
    dual_rows = shard_rows // LANES
    groups_out = OUT_PIECES
    group = shard_rows // groups_out
    cut = group // replicas
    target = point_rows * replicas / shard_rows
    inverse_soft = 1.0 / (features * softness_factor)

    me = lax.axis_index("cent")
    z = lax.axis_index("rep")
    core = me % 2
    xpos = (me // 2) % 2
    ypos = me // 4

    def rel(direction):
        dc, dx, dy = direction % 2, (direction // 2) % 2, direction // 4
        c = 1 - core if dc else core
        x = 1 - xpos if dx else xpos
        y = 1 - ypos if dy else ypos
        return (y * 2 + x) * 2 + c

    peer = [rel(d) for d in range(shards)]
    zpeer = [(z + k) % replicas for k in range(replicas)]

    at_end = jnp.logical_or(z == 0, z == replicas - 1)
    in_mid = jnp.logical_not(at_end)
    partner = z + 1 - 2 * (z % 2)
    low = z // 2
    far_end = 3 - 3 * low
    far_mid = 2 - low

    barrier = pltpu.get_barrier_semaphore()
    for d in range(1, shards):
        pl.semaphore_signal(barrier, inc=1, device_id=(peer[d], z), device_id_type=MESH)
    for k in range(1, replicas):
        pl.semaphore_signal(barrier, inc=1, device_id=(me, zpeer[k]), device_id_type=MESH)
    pl.semaphore_wait(barrier, shards - 1 + replicas - 1)

    mask_copies = []
    for d in range(1, shards):
        copy = pltpu.make_async_remote_copy(
            src_ref=mask_ref.at[peer[d]],
            dst_ref=masks.at[d],
            send_sem=mask_send.at[d],
            recv_sem=mask_recv.at[d],
            device_id=(peer[d], z),
            device_id_type=MESH,
        )
        copy.start()
        mask_copies.append(copy)
    masks[0] = mask_ref[me]

    unit_copies = {}

    def push(slot, chunk, direction):
        rows = pl.ds(chunk * piece, piece)
        copy = pltpu.make_async_remote_copy(
            src_ref=units.at[slot, rows],
            dst_ref=units.at[slot ^ direction, rows],
            send_sem=unit_send.at[slot, chunk, direction // 2],
            recv_sem=unit_recv.at[slot ^ direction, chunk],
            device_id=(peer[direction], z),
            device_id_type=MESH,
        )
        copy.start()
        unit_copies[(slot, chunk, direction)] = copy

    def arrive(slot, chunk):
        rows = pl.ds(chunk * piece, piece)
        pltpu.make_async_copy(
            units.at[slot, rows], units.at[slot, rows], unit_recv.at[slot, chunk]
        ).wait()

    order_x = (0, 1, 2, 3)
    order_y = (2, 3, 0, 1)
    for step in (0, 2, 1, 3):
        rows = pl.ds(step * piece, piece)
        units[0, rows] = normalize(points_ref[rows])
        if step == 0:
            push(0, 0, 2)
        if step == 2:
            push(0, 2, 4)
        if step == 1:
            push(0, 1, 2)
            push(0, 2, 2)
        if step == 3:
            push(0, 3, 4)
            push(0, 3, 2)
            push(0, 0, 4)
            push(0, 1, 4)
    for step in range(pieces):
        push(0, step, 1)

    cunit[...] = normalize(centroids_ref[...])

    def block_kernel(slot, start=0, count=shard_rows):
        scores = lax.dot_general(
            cunit[pl.ds(start, count), :],
            units[slot],
            (((1,), (1,)), ((), ())),
            preferred_element_type=jnp.float32,
        )
        marks = masks[slot]
        for b in range(count // span):
            rows = pl.ds(start + b * span, span)
            mark = marks[start // span + b : start // span + b + 1, :]
            kern[slot, rows, :] = (
                jnp.exp(scores[b * span : (b + 1) * span] * inverse_soft) * mark
            )

    block_kernel(0)
    for step in range(pieces):
        tx, ty = order_x[step], order_y[step]
        arrive(2, tx)
        if step < 2:
            push(2, tx, 4)
        push(2, tx, 1)
        arrive(4, ty)
        if step < 2:
            push(4, ty, 2)
        push(4, ty, 1)
        if step == 1:
            for copy in mask_copies:
                copy.wait()
            for chunk in range(pieces):
                arrive(1, chunk)
            block_kernel(1)
        if step >= 2:
            arrive(6, order_x[step - 2])
            push(6, order_x[step - 2], 1)
            arrive(6, order_y[step - 2])
            push(6, order_y[step - 2], 1)
    for slot in (2, 4, 6, 3, 5, 7):
        if slot % 2:
            for chunk in range(pieces):
                arrive(slot, chunk)
        block_kernel(slot)
    for copy in unit_copies.values():
        copy.wait_send()

    duals_now = duals_ref[...]
    groups = shard_rows // SUBLANES
    tiles = point_rows // LANES

    def spread_scale(scaling):
        for t in range(dual_rows):
            row = jnp.broadcast_to(scaling[t : t + 1, :], (LANES, LANES))
            scale_cols[pl.ds(t * LANES, LANES), :] = row.T

    def row_pass():
        def step(g, acc):
            rows = pl.ds(pl.multiple_of(g * SUBLANES, SUBLANES), SUBLANES)
            wide = jnp.concatenate([scale_cols[rows, :]] * tiles, axis=1)
            return tuple(acc[p] + kern[p, rows, :] * wide for p in range(shards))

        zero = jnp.zeros((SUBLANES, point_rows), jnp.float32)
        acc = lax.fori_loop(0, groups, step, (zero,) * shards, unroll=2)
        return jnp.concatenate([jnp.sum(a, axis=0, keepdims=True) for a in acc], axis=0)

    def col_pass(inverse):
        wide = [
            jnp.broadcast_to(inverse[p : p + 1, :], (SUBLANES, point_rows)) for p in range(shards)
        ]

        def step(g, carry):
            rows = pl.ds(pl.multiple_of(g * SUBLANES, SUBLANES), SUBLANES)
            total = kern[0, rows, :] * wide[0]
            for p in range(1, shards):
                total = total + kern[p, rows, :] * wide[p]
            narrow = total[:, :LANES]
            for t in range(1, tiles):
                narrow = narrow + total[:, t * LANES : (t + 1) * LANES]
            mass_cols[rows, :] = narrow
            return carry

        lax.fori_loop(0, groups, step, 0, unroll=2)
        parts = [
            jnp.sum(mass_cols[pl.ds(t * LANES, LANES), :].T, axis=0, keepdims=True)
            for t in range(dual_rows)
        ]
        return jnp.concatenate(parts * (SUBLANES // dual_rows), axis=0)

    def row_exchange(turn, part):
        row_parts[turn, 0] = part
        copies = []
        for d in (6, 7, 2, 4, 3, 5, 1):
            copy = pltpu.make_async_remote_copy(
                src_ref=row_parts.at[turn, 0],
                dst_ref=row_parts.at[turn, d],
                send_sem=row_send.at[turn, d],
                recv_sem=row_recv.at[turn, d],
                device_id=(peer[d], z),
                device_id_type=MESH,
            )
            copy.start()
            copies.append(copy)
        for copy in copies:
            copy.wait()
        rows = []
        for p in range(shards):
            total = part[p : p + 1, :]
            for d in range(1, shards):
                total = total + row_parts[turn, d, pl.ds(p ^ d, 1), :]
            rows.append(total)
        return jnp.concatenate(rows, axis=0)

    def col_exchange(turn, part):
        col_parts[turn, z] = part
        copies = []
        for k in range(1, replicas):
            copy = pltpu.make_async_remote_copy(
                src_ref=col_parts.at[turn, z],
                dst_ref=col_parts.at[turn, z],
                send_sem=col_send.at[turn, k],
                recv_sem=col_recv.at[turn, k],
                device_id=(me, zpeer[k]),
                device_id_type=MESH,
            )
            copy.start()
            copies.append(copy)
        for copy in copies:
            copy.wait()
        total = col_parts[turn, 0]
        for k in range(1, replicas):
            total = total + col_parts[turn, k]
        return total

    row_turn = 0
    col_turn = 0
    for loop_counter in range(ITERS):
        last = loop_counter == ITERS - 1
        for turn_index in range(SINK + 1):
            scaling = jnp.exp(duals_now)
            spread_scale(scaling)
            inverse = 1.0 / row_exchange(row_turn, row_pass())
            row_turn += 1
            if turn_index < SINK:
                mass = col_exchange(col_turn, col_pass(inverse) * scaling)
                col_turn += 1
                duals_now = duals_now + jnp.log(2.0 * target) - jnp.log(mass + target)

        row_parts[row_turn - 1, 0] = inverse

        dest = out_ref if last else cunit

        def part_rows(i, q):
            start = i * group + q * cut
            if not isinstance(q, int):
                start = pl.multiple_of(start, cut)
            return pl.ds(start, cut)

        def sum_copy(i, source, landing, to):
            return pltpu.make_async_remote_copy(
                src_ref=sums_out.at[loop_counter, i, source],
                dst_ref=sums_in.at[loop_counter, i, landing],
                send_sem=sum_send.at[loop_counter, i, source],
                recv_sem=sum_recv.at[loop_counter, i, landing],
                device_id=(me, to),
                device_id_type=MESH,
            )

        def sum_arrive(i, landing):
            ref = sums_in.at[loop_counter, i, landing]
            pltpu.make_async_copy(ref, ref, sum_recv.at[loop_counter, i, landing]).wait()
            return sums_in[loop_counter, i, landing].astype(jnp.float32)

        def new_copy(i, q, to, number):
            return pltpu.make_async_remote_copy(
                src_ref=dest.at[part_rows(i, q)],
                dst_ref=dest.at[part_rows(i, q)],
                send_sem=new_send.at[loop_counter, i, number],
                recv_sem=new_recv.at[loop_counter, i, q],
                device_id=(me, to),
                device_id_type=MESH,
            )

        def new_arrive(i, q):
            ref = dest.at[part_rows(i, q)]
            pltpu.make_async_copy(ref, ref, new_recv.at[loop_counter, i, q]).wait()

        def accumulate(i):
            rows = pl.ds(i * group, group)
            wide = jnp.concatenate([scale_cols[rows, :]] * tiles, axis=1)

            def step(slot, acc):
                inv = row_parts[row_turn - 1, 0, pl.ds(slot, 1), :]
                weights = (inv * kern[slot, rows, :] * wide).astype(jnp.bfloat16)
                return acc + jnp.dot(weights, units[slot], preferred_element_type=jnp.float32)

            zero = jnp.zeros((group, features), jnp.float32)
            sums[rows, :] = lax.fori_loop(0, shards, step, zero)

            def raw(source, q):
                sums_out[loop_counter, i, source] = sums[part_rows(i, q), :].astype(jnp.bfloat16)
                sum_copy(i, source, source, partner).start()

            @pl.when(at_end)
            def _():
                raw(2, far_end)
                raw(3, far_mid)

            raw(0, partner)

        def pair_sums(i):
            @pl.when(in_mid)
            def _():
                for source, q in ((2, far_end), (3, far_mid)):
                    total = sum_arrive(i, source) + sums[part_rows(i, q), :]
                    sums_out[loop_counter, i, source] = total.astype(jnp.bfloat16)
                    sum_copy(i, source, 1, q).start()

        def finish_sums(i):
            mine = part_rows(i, z)
            total = sums[mine, :] + sum_arrive(i, 0)
            fresh = normalize(total + sum_arrive(i, 1))
            dest[mine, :] = fresh if last else normalize(fresh)
            new_copy(i, z, far_mid, 1).start()
            new_copy(i, z, partner, 0).start()

        def forward_new(i):
            @pl.when(in_mid)
            def _():
                for number, q in ((3, far_mid), (2, far_end)):
                    new_arrive(i, q)
                    new_copy(i, q, partner, number).start()

            new_arrive(i, partner)

        def end_new(i):
            @pl.when(at_end)
            def _():
                new_arrive(i, far_mid)
                new_arrive(i, far_end)

        def remake(i):
            if last:
                return

            def step(slot, carry):
                block_kernel(slot, i * group, group)
                return carry

            lax.fori_loop(0, shards, step, 0)

        stages = (accumulate, pair_sums, finish_sums, forward_new, end_new, remake)
        lags = (0, 1, 2, 3, 4, 4)
        for step in range(groups_out + lags[-1]):
            for lag, stage in zip(lags, stages):
                if 0 <= step - lag < groups_out:
                    stage(step - lag)
        for i in range(groups_out):
            for source in (0, 2, 3):
                sum_copy(i, source, source, partner).wait_send()
            new_copy(i, z, partner, 0).wait_send()
            new_copy(i, z, far_mid, 1).wait_send()

            @pl.when(in_mid)
            def _():
                new_copy(i, far_end, partner, 2).wait_send()
                new_copy(i, far_mid, partner, 3).wait_send()

    duals_out_ref[...] = duals_now


def fused_body(points, centroids, owners, blocks, duals):
    point_rows, features = points.shape
    shard_rows = centroids.shape[0]
    shards = lax.axis_size("cent")
    replicas = lax.axis_size("rep")
    dims = (shards, replicas, point_rows, shard_rows, features)
    dual_rows = shard_rows // LANES
    cut = shard_rows // (OUT_PIECES * replicas)
    wanted = owners.T[None, None, :, None, :] == jnp.arange(shards, dtype=jnp.int32).reshape(
        -1, 1, 1, 1, 1
    )
    named = jnp.transpose(blocks, (1, 2, 0))[None, None] == jnp.arange(
        BLOCKS_DEV, dtype=jnp.int32
    ).reshape(1, -1, 1, 1, 1)
    mask = jnp.any(jnp.logical_and(wanted, named), axis=(2, 3)).astype(jnp.float32)
    dual_tile = jnp.concatenate([duals.reshape(dual_rows, LANES)] * (SUBLANES // dual_rows), axis=0)
    vmem = pl.BlockSpec(memory_space=pltpu.VMEM)
    row_turns = ITERS * (SINK + 1)
    col_turns = ITERS * SINK
    dma = pltpu.SemaphoreType.DMA
    new_centroids, duals_out = pl.pallas_call(
        functools.partial(fused_kernel, dims),
        out_shape=(
            jax.ShapeDtypeStruct((shard_rows, features), jnp.bfloat16),
            jax.ShapeDtypeStruct((SUBLANES, LANES), jnp.float32),
        ),
        in_specs=[vmem] * 4,
        out_specs=(vmem, vmem),
        scratch_shapes=[
            pltpu.VMEM((shards, point_rows, features), jnp.bfloat16),
            pltpu.VMEM((shards, BLOCKS_DEV, point_rows), jnp.float32),
            pltpu.VMEM((shards, shard_rows, point_rows), jnp.float32),
            pltpu.VMEM((shard_rows, features), jnp.bfloat16),
            pltpu.VMEM((shard_rows, LANES), jnp.float32),
            pltpu.VMEM((shard_rows, LANES), jnp.float32),
            pltpu.VMEM((shard_rows, features), jnp.float32),
            pltpu.VMEM((row_turns, shards, shards, point_rows), jnp.float32),
            pltpu.VMEM((col_turns, replicas, SUBLANES, LANES), jnp.float32),
            pltpu.VMEM((ITERS, OUT_PIECES, 4, cut, features), jnp.bfloat16),
            pltpu.VMEM((ITERS, OUT_PIECES, 4, cut, features), jnp.bfloat16),
            dma((shards, 4, 3)),
            dma((shards, 4)),
            dma((shards,)),
            dma((shards,)),
            dma((row_turns, shards)),
            dma((row_turns, shards)),
            dma((col_turns, replicas)),
            dma((col_turns, replicas)),
            dma((ITERS, OUT_PIECES, 4)),
            dma((ITERS, OUT_PIECES, 4)),
            dma((ITERS, OUT_PIECES, 4)),
            dma((ITERS, OUT_PIECES, 4)),
        ],
        compiler_params=pltpu.CompilerParams(
            collective_id=0, has_side_effects=True, vmem_limit_bytes=VMEM_LIMIT
        ),
        name="fused_kmeans",
    )(points, centroids, mask, dual_tile)
    return new_centroids, duals_out[:dual_rows].reshape(shard_rows)


def solution(mesh):
    shards = mesh.shape["cent"]

    def body(points, centroids, owners, blocks, duals):
        point_rows, features = points.shape
        shard_rows = centroids.shape[0]
        plane_bytes = shards * point_rows * (2 * features + 4 * shard_rows)
        cube = shards == 2**3 and mesh.shape["rep"] == 2 * 2 and shard_rows % LANES == 0 and SUBLANES % (shard_rows // LANES) == 0
        if cube and plane_bytes <= VMEM_LIMIT // 3:
            return fused_body(points, centroids, owners, blocks, duals)
        return routed_body(points, centroids, owners, blocks, duals)

    return jax.shard_map(
        body,
        mesh=mesh,
        in_specs=(
            P(("cent", "rep"), None),
            P("cent", None),
            P(("cent", "rep"), None),
            P(("cent", "rep"), None, None),
            P("cent"),
        ),
        out_specs=(P("cent", None), P("cent")),
        check_vma=False,
    )
```

```python
import functools

import jax
import jax.numpy as jnp
from jax import lax
from jax.experimental import pallas as pl
from jax.experimental.pallas import tpu as pltpu
from jax.sharding import PartitionSpec as P

BLOCKS_DEV = 8
CAND = 4
SINK = 3
ITERS = 2
LANES = 128
SUBLANES = 8
OUT_PIECES = 4
MESH = pl.DeviceIdType.MESH
VMEM_LIMIT = 64000000


softness_factor = 0.02
EPSILON = 1e-06


def normalize(values):
    widened = values.astype(jnp.float32)
    return (
        widened * lax.rsqrt(jnp.mean(widened * widened, axis=-1, keepdims=True) + EPSILON)
    ).astype(jnp.bfloat16)


def candidate_mask(labels_in, block_span):
    member = jnp.any(
        labels_in[:, :, None] == jnp.arange(BLOCKS_DEV, dtype=jnp.int32)[None, None, :], axis=1
    )
    return jnp.repeat(member.astype(jnp.float32), block_span, axis=1)


def kernel_of(slot_rows, slot_mask, centroid_unit, feature_dimension):
    affinity_scores = lax.dot_general(
        slot_rows, centroid_unit, (((1,), (1,)), ((), ())), preferred_element_type=jnp.float32
    ) / (feature_dimension * softness_factor)
    return jnp.exp(affinity_scores) * slot_mask


def routed_body(points, centroids, owners, blocks, duals):
    point_rows, feature_dimension = points.shape
    shard_rows = centroids.shape[0]
    shards = lax.axis_size("cent")
    replicas = lax.axis_size("rep")
    routes = owners.shape[1]
    capacity = 5 * point_rows // shards
    block_span = shard_rows // BLOCKS_DEV
    target = point_rows * replicas / shard_rows
    unit_rows = normalize(points)
    flat_owner = owners.reshape(-1)
    flat_point = jnp.arange(point_rows * routes, dtype=jnp.int32) // routes
    onehot = (flat_owner[:, None] == jnp.arange(shards, dtype=jnp.int32)[None, :]).astype(jnp.int32)
    position = jnp.sum((jnp.cumsum(onehot, axis=0) - onehot) * onehot, axis=1)
    outgoing = (
        jnp.zeros((shards, capacity, feature_dimension), jnp.bfloat16)
        .at[flat_owner, position]
        .set(unit_rows[flat_point])
    )
    labels = (
        jnp.full((shards, capacity, CAND), -1, jnp.int32)
        .at[flat_owner, position]
        .set(blocks.reshape(-1, CAND))
    )
    first_unit = normalize(centroids)
    received_rows = (
        lax.all_to_all(outgoing, "cent", split_axis=0, concat_axis=0, tiled=True),
        lax.all_to_all(labels, "cent", split_axis=0, concat_axis=0, tiled=True),
    )
    slot_rows = received_rows[0].reshape(-1, feature_dimension)
    slot_mask = candidate_mask(received_rows[1].reshape(-1, CAND), block_span)
    first_kernel = kernel_of(slot_rows, slot_mask, first_unit, feature_dimension)
    current = centroids
    duals_now = duals
    for loop_counter in range(ITERS):
        if loop_counter == 0:
            kernel = first_kernel
        else:
            kernel = kernel_of(slot_rows, slot_mask, normalize(current), feature_dimension)
        for turn_index in range(SINK + 1):
            scaling = jnp.exp(duals_now)
            partial_rows = jnp.dot(kernel, scaling, precision=lax.Precision.HIGHEST).reshape(
                shards, capacity
            )
            returned = lax.all_to_all(partial_rows, "cent", split_axis=0, concat_axis=0, tiled=True)
            totals = jnp.sum(returned[flat_owner, position].reshape(point_rows, routes), axis=1)
            inverse = 1.0 / totals
            spread = (
                jnp.zeros((shards, capacity), jnp.float32)
                .at[flat_owner, position]
                .set(inverse[flat_point])
            )
            row_scale = lax.all_to_all(
                spread, "cent", split_axis=0, concat_axis=0, tiled=True
            ).reshape(-1)
            if turn_index < SINK:
                local_mass = jnp.dot(row_scale, kernel, precision=lax.Precision.HIGHEST) * scaling
                column_mass = lax.psum(local_mass, "rep")
                duals_now = duals_now + jnp.log(2.0 * target) - jnp.log(column_mass + target)
        weights = (row_scale[:, None] * kernel * scaling[None, :]).astype(jnp.bfloat16)
        share_sums = lax.psum_scatter(
            lax.dot_general(
                weights, slot_rows, (((0,), (0,)), ((), ())), preferred_element_type=jnp.float32
            ),
            "rep",
            scatter_dimension=0,
            tiled=True,
        )
        current = lax.all_gather(normalize(share_sums), "rep", axis=0, tiled=True)
    return (current, duals_now)


def fused_kernel(
    dims,
    points_ref,
    centroids_ref,
    mask_ref,
    duals_ref,
    out_ref,
    duals_out_ref,
    units,
    masks,
    kern,
    cunit,
    scale_cols,
    mass_cols,
    sums,
    row_parts,
    col_parts,
    sums_out,
    sums_in,
    unit_send,
    unit_recv,
    mask_send,
    mask_recv,
    row_send,
    row_recv,
    col_send,
    col_recv,
    sum_send,
    sum_recv,
    new_send,
    new_recv,
):
    shards, replicas, point_rows, shard_rows, features = dims
    span = shard_rows // BLOCKS_DEV
    pieces = 4
    piece = point_rows // pieces
    dual_rows = shard_rows // LANES
    groups_out = OUT_PIECES
    group = shard_rows // groups_out
    cut = group // replicas
    target = point_rows * replicas / shard_rows
    inverse_soft = 1.0 / (features * softness_factor)

    me = lax.axis_index("cent")
    z = lax.axis_index("rep")
    core = me % 2
    xpos = (me // 2) % 2
    ypos = me // 4

    def rel(direction):
        dc, dx, dy = direction % 2, (direction // 2) % 2, direction // 4
        c = 1 - core if dc else core
        x = 1 - xpos if dx else xpos
        y = 1 - ypos if dy else ypos
        return (y * 2 + x) * 2 + c

    peer = [rel(d) for d in range(shards)]
    zpeer = [(z + k) % replicas for k in range(replicas)]

    at_end = jnp.logical_or(z == 0, z == replicas - 1)
    in_mid = jnp.logical_not(at_end)
    partner = z + 1 - 2 * (z % 2)
    low = z // 2
    far_end = 3 - 3 * low
    far_mid = 2 - low

    barrier = pltpu.get_barrier_semaphore()
    for d in range(1, shards):
        pl.semaphore_signal(barrier, inc=1, device_id=(peer[d], z), device_id_type=MESH)
    for k in range(1, replicas):
        pl.semaphore_signal(barrier, inc=1, device_id=(me, zpeer[k]), device_id_type=MESH)
    pl.semaphore_wait(barrier, shards - 1 + replicas - 1)

    mask_copies = []
    for d in range(1, shards):
        copy = pltpu.make_async_remote_copy(
            src_ref=mask_ref.at[peer[d]],
            dst_ref=masks.at[d],
            send_sem=mask_send.at[d],
            recv_sem=mask_recv.at[d],
            device_id=(peer[d], z),
            device_id_type=MESH,
        )
        copy.start()
        mask_copies.append(copy)
    masks[0] = mask_ref[me]

    unit_copies = {}

    def push(slot, chunk, direction):
        rows = pl.ds(chunk * piece, piece)
        copy = pltpu.make_async_remote_copy(
            src_ref=units.at[slot, rows],
            dst_ref=units.at[slot ^ direction, rows],
            send_sem=unit_send.at[slot, chunk, direction // 2],
            recv_sem=unit_recv.at[slot ^ direction, chunk],
            device_id=(peer[direction], z),
            device_id_type=MESH,
        )
        copy.start()
        unit_copies[(slot, chunk, direction)] = copy

    def arrive(slot, chunk):
        rows = pl.ds(chunk * piece, piece)
        pltpu.make_async_copy(
            units.at[slot, rows], units.at[slot, rows], unit_recv.at[slot, chunk]
        ).wait()

    order_x = (0, 1, 2, 3)
    order_y = (2, 3, 0, 1)
    for step in (0, 2, 1, 3):
        rows = pl.ds(step * piece, piece)
        units[0, rows] = normalize(points_ref[rows])
        if step == 0:
            push(0, 0, 2)
        if step == 2:
            push(0, 2, 4)
        if step == 1:
            push(0, 1, 2)
            push(0, 2, 2)
        if step == 3:
            push(0, 3, 4)
            push(0, 3, 2)
            push(0, 0, 4)
            push(0, 1, 4)
    for step in range(pieces):
        push(0, step, 1)

    cunit[...] = normalize(centroids_ref[...])

    def block_kernel(slot, start=0, count=shard_rows, first=0, width=point_rows):
        held = pl.ds(first, width)
        scores = lax.dot_general(
            cunit[pl.ds(start, count), :],
            units[slot, held, :],
            (((1,), (1,)), ((), ())),
            preferred_element_type=jnp.float32,
        )
        marks = masks[slot, :, held]
        for b in range(count // span):
            rows = pl.ds(start + b * span, span)
            mark = marks[start // span + b : start // span + b + 1, :]
            kern[slot, rows, held] = (
                jnp.exp(scores[b * span : (b + 1) * span] * inverse_soft) * mark
            )

    def half_kernels(halves):
        for slot, chunks in halves:
            block_kernel(slot, first=min(chunks) * piece, width=2 * piece)

    block_kernel(0)
    for step in range(pieces):
        tx, ty = order_x[step], order_y[step]
        arrive(2, tx)
        if step < 2:
            push(2, tx, 4)
        push(2, tx, 1)
        arrive(4, ty)
        if step < 2:
            push(4, ty, 2)
        push(4, ty, 1)
        if step == 1:
            for copy in mask_copies:
                copy.wait()
            for chunk in range(pieces):
                arrive(1, chunk)
            block_kernel(1)
        if step >= 2:
            arrive(6, order_x[step - 2])
            push(6, order_x[step - 2], 1)
            arrive(6, order_y[step - 2])
            push(6, order_y[step - 2], 1)
        if step == 2:
            for slot, chunks in ((3, order_x[:2]), (5, order_y[:2])):
                for chunk in chunks:
                    arrive(slot, chunk)
            half_kernels(((2, order_x[:2]), (4, order_y[:2]), (3, order_x[:2]), (5, order_y[:2])))
    half_kernels(((2, order_x[2:]), (4, order_y[2:])))
    for slot, chunks in ((3, order_x[2:]), (5, order_y[2:])):
        for chunk in chunks:
            arrive(slot, chunk)
        half_kernels(((slot, chunks),))
    half_kernels(((6, order_x[:2]), (6, order_y[:2])))
    for chunk in range(pieces):
        arrive(7, chunk)
    half_kernels(((7, order_x[:2]), (7, order_y[:2])))
    for copy in unit_copies.values():
        copy.wait_send()

    duals_now = jnp.concatenate([duals_ref[...]] * (SUBLANES // dual_rows), axis=0)
    groups = shard_rows // SUBLANES
    tiles = point_rows // LANES

    def spread_scale(scaling):
        for t in range(dual_rows):
            row = jnp.broadcast_to(scaling[t : t + 1, :], (LANES, LANES))
            scale_cols[pl.ds(t * LANES, LANES), :] = row.T

    def row_pass():
        def step(g, acc):
            rows = pl.ds(pl.multiple_of(g * SUBLANES, SUBLANES), SUBLANES)
            wide = jnp.concatenate([scale_cols[rows, :]] * tiles, axis=1)
            return tuple(acc[p] + kern[p, rows, :] * wide for p in range(shards))

        zero = jnp.zeros((SUBLANES, point_rows), jnp.float32)
        acc = lax.fori_loop(0, groups, step, (zero,) * shards, unroll=2)
        return jnp.concatenate([jnp.sum(a, axis=0, keepdims=True) for a in acc], axis=0)

    def col_pass(inverse):
        wide = [
            jnp.broadcast_to(inverse[p : p + 1, :], (SUBLANES, point_rows)) for p in range(shards)
        ]

        def step(g, carry):
            rows = pl.ds(pl.multiple_of(g * SUBLANES, SUBLANES), SUBLANES)
            total = kern[0, rows, :] * wide[0]
            for p in range(1, shards):
                total = total + kern[p, rows, :] * wide[p]
            narrow = total[:, :LANES]
            for t in range(1, tiles):
                narrow = narrow + total[:, t * LANES : (t + 1) * LANES]
            mass_cols[rows, :] = narrow
            return carry

        lax.fori_loop(0, groups, step, 0, unroll=2)
        parts = [
            jnp.sum(mass_cols[pl.ds(t * LANES, LANES), :].T, axis=0, keepdims=True)
            for t in range(dual_rows)
        ]
        return jnp.concatenate(parts * (SUBLANES // dual_rows), axis=0)

    def row_exchange(turn, part):
        row_parts[turn, 0] = part
        copies = []
        for d in (6, 7, 2, 4, 3, 5, 1):
            copy = pltpu.make_async_remote_copy(
                src_ref=row_parts.at[turn, 0],
                dst_ref=row_parts.at[turn, d],
                send_sem=row_send.at[turn, d],
                recv_sem=row_recv.at[turn, d],
                device_id=(peer[d], z),
                device_id_type=MESH,
            )
            copy.start()
            copies.append(copy)
        for copy in copies:
            copy.wait()
        rows = []
        for p in range(shards):
            total = part[p : p + 1, :]
            for d in range(1, shards):
                total = total + row_parts[turn, d, pl.ds(p ^ d, 1), :]
            rows.append(total)
        return jnp.concatenate(rows, axis=0)

    def col_exchange(turn, part):
        col_parts[turn, z] = part
        copies = []
        for k in range(1, replicas):
            copy = pltpu.make_async_remote_copy(
                src_ref=col_parts.at[turn, z],
                dst_ref=col_parts.at[turn, z],
                send_sem=col_send.at[turn, k],
                recv_sem=col_recv.at[turn, k],
                device_id=(me, zpeer[k]),
                device_id_type=MESH,
            )
            copy.start()
            copies.append(copy)
        for copy in copies:
            copy.wait()
        total = col_parts[turn, 0]
        for k in range(1, replicas):
            total = total + col_parts[turn, k]
        return total

    row_turn = 0
    col_turn = 0
    for loop_counter in range(ITERS):
        last = loop_counter == ITERS - 1
        for turn_index in range(SINK + 1):
            scaling = jnp.exp(duals_now)
            spread_scale(scaling)
            inverse = 1.0 / row_exchange(row_turn, row_pass())
            row_turn += 1
            if turn_index < SINK:
                mass = col_exchange(col_turn, col_pass(inverse) * scaling)
                col_turn += 1
                duals_now = duals_now + jnp.log(2.0 * target) - jnp.log(mass + target)

        row_parts[row_turn - 1, 0] = inverse

        dest = out_ref if last else cunit

        def part_rows(i, q):
            start = i * group + q * cut
            if not isinstance(q, int):
                start = pl.multiple_of(start, cut)
            return pl.ds(start, cut)

        def sum_copy(i, source, landing, to):
            return pltpu.make_async_remote_copy(
                src_ref=sums_out.at[loop_counter, i, source],
                dst_ref=sums_in.at[loop_counter, i, landing],
                send_sem=sum_send.at[loop_counter, i, source],
                recv_sem=sum_recv.at[loop_counter, i, landing],
                device_id=(me, to),
                device_id_type=MESH,
            )

        def sum_arrive(i, landing):
            ref = sums_in.at[loop_counter, i, landing]
            pltpu.make_async_copy(ref, ref, sum_recv.at[loop_counter, i, landing]).wait()
            return sums_in[loop_counter, i, landing].astype(jnp.float32)

        def new_copy(i, q, to, number):
            return pltpu.make_async_remote_copy(
                src_ref=dest.at[part_rows(i, q)],
                dst_ref=dest.at[part_rows(i, q)],
                send_sem=new_send.at[loop_counter, i, number],
                recv_sem=new_recv.at[loop_counter, i, q],
                device_id=(me, to),
                device_id_type=MESH,
            )

        def new_arrive(i, q):
            ref = dest.at[part_rows(i, q)]
            pltpu.make_async_copy(ref, ref, new_recv.at[loop_counter, i, q]).wait()

        def accumulate(i):
            rows = pl.ds(i * group, group)
            wide = jnp.concatenate([scale_cols[rows, :]] * tiles, axis=1)

            def step(slot, acc):
                inv = row_parts[row_turn - 1, 0, pl.ds(slot, 1), :]
                weights = (inv * kern[slot, rows, :] * wide).astype(jnp.bfloat16)
                return acc + jnp.dot(weights, units[slot], preferred_element_type=jnp.float32)

            zero = jnp.zeros((group, features), jnp.float32)
            sums[rows, :] = lax.fori_loop(0, shards, step, zero)

            def raw(source, q):
                sums_out[loop_counter, i, source] = sums[part_rows(i, q), :].astype(jnp.bfloat16)
                sum_copy(i, source, source, partner).start()

            @pl.when(at_end)
            def _():
                raw(2, far_end)
                raw(3, far_mid)

            raw(0, partner)

        def pair_sums(i):
            @pl.when(in_mid)
            def _():
                for source, q in ((2, far_end), (3, far_mid)):
                    total = sum_arrive(i, source) + sums[part_rows(i, q), :]
                    sums_out[loop_counter, i, source] = total.astype(jnp.bfloat16)
                    sum_copy(i, source, 1, q).start()

        def finish_sums(i):
            mine = part_rows(i, z)
            total = sums[mine, :] + sum_arrive(i, 0)
            fresh = normalize(total + sum_arrive(i, 1))
            dest[mine, :] = fresh if last else normalize(fresh)
            new_copy(i, z, far_mid, 1).start()
            new_copy(i, z, partner, 0).start()

        def forward_new(i):
            @pl.when(in_mid)
            def _():
                for number, q in ((3, far_mid), (2, far_end)):
                    new_arrive(i, q)
                    new_copy(i, q, partner, number).start()

            new_arrive(i, partner)

        def end_new(i):
            @pl.when(at_end)
            def _():
                new_arrive(i, far_mid)
                new_arrive(i, far_end)

        def remake(i):
            if last:
                return

            def step(slot, carry):
                block_kernel(slot, i * group, group)
                return carry

            lax.fori_loop(0, shards, step, 0)

        stages = (accumulate, pair_sums, finish_sums, forward_new, end_new, remake)
        lags = (0, 1, 2, 3, 4, 4)
        for step in range(groups_out + lags[-1]):
            for lag, stage in zip(lags, stages):
                if 0 <= step - lag < groups_out:
                    stage(step - lag)
        for i in range(groups_out):
            for source in (0, 2, 3):
                sum_copy(i, source, source, partner).wait_send()
            new_copy(i, z, partner, 0).wait_send()
            new_copy(i, z, far_mid, 1).wait_send()

            @pl.when(in_mid)
            def _():
                new_copy(i, far_end, partner, 2).wait_send()
                new_copy(i, far_mid, partner, 3).wait_send()

    duals_out_ref[...] = duals_now[:dual_rows]


def fused_body(points, centroids, owners, blocks, duals):
    point_rows, features = points.shape
    shard_rows = centroids.shape[0]
    shards = lax.axis_size("cent")
    replicas = lax.axis_size("rep")
    dims = (shards, replicas, point_rows, shard_rows, features)
    dual_rows = shard_rows // LANES
    cut = shard_rows // (OUT_PIECES * replicas)
    wanted = owners.T[None, None, :, None, :] == jnp.arange(shards, dtype=jnp.int32).reshape(
        -1, 1, 1, 1, 1
    )
    named = jnp.transpose(blocks, (1, 2, 0))[None, None] == jnp.arange(
        BLOCKS_DEV, dtype=jnp.int32
    ).reshape(1, -1, 1, 1, 1)
    mask = jnp.any(jnp.logical_and(wanted, named), axis=(2, 3)).astype(jnp.float32)
    dual_tile = duals.reshape(dual_rows, LANES)
    vmem = pl.BlockSpec(memory_space=pltpu.VMEM)
    row_turns = ITERS * (SINK + 1)
    col_turns = ITERS * SINK
    dma = pltpu.SemaphoreType.DMA
    new_centroids, duals_out = pl.pallas_call(
        functools.partial(fused_kernel, dims),
        out_shape=(
            jax.ShapeDtypeStruct((shard_rows, features), jnp.bfloat16),
            jax.ShapeDtypeStruct((dual_rows, LANES), jnp.float32),
        ),
        in_specs=[vmem] * 4,
        out_specs=(vmem, vmem),
        scratch_shapes=[
            pltpu.VMEM((shards, point_rows, features), jnp.bfloat16),
            pltpu.VMEM((shards, BLOCKS_DEV, point_rows), jnp.float32),
            pltpu.VMEM((shards, shard_rows, point_rows), jnp.float32),
            pltpu.VMEM((shard_rows, features), jnp.bfloat16),
            pltpu.VMEM((shard_rows, LANES), jnp.float32),
            pltpu.VMEM((shard_rows, LANES), jnp.float32),
            pltpu.VMEM((shard_rows, features), jnp.float32),
            pltpu.VMEM((row_turns, shards, shards, point_rows), jnp.float32),
            pltpu.VMEM((col_turns, replicas, SUBLANES, LANES), jnp.float32),
            pltpu.VMEM((ITERS, OUT_PIECES, 4, cut, features), jnp.bfloat16),
            pltpu.VMEM((ITERS, OUT_PIECES, 4, cut, features), jnp.bfloat16),
            dma((shards, 4, 3)),
            dma((shards, 4)),
            dma((shards,)),
            dma((shards,)),
            dma((row_turns, shards)),
            dma((row_turns, shards)),
            dma((col_turns, replicas)),
            dma((col_turns, replicas)),
            dma((ITERS, OUT_PIECES, 4)),
            dma((ITERS, OUT_PIECES, 4)),
            dma((ITERS, OUT_PIECES, 4)),
            dma((ITERS, OUT_PIECES, 4)),
        ],
        compiler_params=pltpu.CompilerParams(
            collective_id=0, has_side_effects=True, vmem_limit_bytes=VMEM_LIMIT
        ),
        name="fused_kmeans",
    )(points, centroids, mask, dual_tile)
    return new_centroids, duals_out.reshape(shard_rows)


def solution(mesh):
    shards = mesh.shape["cent"]

    def body(points, centroids, owners, blocks, duals):
        point_rows, features = points.shape
        shard_rows = centroids.shape[0]
        plane_bytes = shards * point_rows * (2 * features + 4 * shard_rows)
        cube = shards == 2**3 and mesh.shape["rep"] == 2 * 2 and shard_rows % LANES == 0 and SUBLANES % (shard_rows // LANES) == 0
        if cube and plane_bytes <= VMEM_LIMIT // 3:
            return fused_body(points, centroids, owners, blocks, duals)
        return routed_body(points, centroids, owners, blocks, duals)

    return jax.shard_map(
        body,
        mesh=mesh,
        in_specs=(
            P(("cent", "rep"), None),
            P("cent", None),
            P(("cent", "rep"), None),
            P(("cent", "rep"), None, None),
            P("cent"),
        ),
        out_specs=(P("cent", None), P("cent")),
        check_vma=False,
    )
```
